512 devices in a mesh: rep: 2 (over x_hi), row: 8 (over y, x_lo), col: 32 (over z, core).
Axes of the slice: x: 4 (x_hi: 2, x_lo: 2; x = x_hi * 2 + x_lo), y: 4, z: 16, core: 2. Of those that a mesh axis runs over, the one named last changes fastest.
Arguments:
- tokens: bfloat16 [2, 32, 256, 2048], P('rep', 'col', None, 'row'), may hold values from -6 to 6
- w_qkv: bfloat16 [2048, 3, 2048], P('col', None, 'row'), may hold values from -0.125 to 0.125
- w_out: bfloat16 [2048, 2048], P('row', 'col'), may hold values from -0.125 to 0.125
- w_up: bfloat16 [2048, 8192], P('col', 'row'), may hold values from -0.125 to 0.125
- w_down: bfloat16 [8192, 2048], P('row', 'col'), may hold values from -0.0625 to 0.0625
- ln1_gain: float32 [2048], replicated, may hold values from 0.25 to 1.75
- ln2_gain: float32 [2048], replicated, may hold values from 0.25 to 1.75
- kv_pool: bfloat16 [2, 2, 256, 128, 2048], P('rep', None, 'col', None, 'row'), may hold values from -240 to 240
- page_table: int32 [2, 32, 8], P(None, 'col'), may hold values from 0 to 7, as said below
- lengths: int32 [2, 32], P(None, 'col'), may hold values from 1 to 1024, as said below
- moved: int32 [32], P('col'), may hold values 0 or 1
Outputs:
- layer_out: bfloat16 [2, 32, 256, 2048], P('rep', 'col', None, 'row')
The draws below stay inside these ranges and needn't reach their ends.
Inputs may be any that keep to these rules, and one draw needn't show every extreme that they name: `page_table`: within each block of 1 slots of one replica, the page entries are a permutation of 0 to 7. `lengths`: some slot's cache holds the full 8 * 128 tokens.
All inputs are finite; a program needn't handle non-finite values. No bound on the sum of `moved` on one device may be relied on, other than what follows from the above.
Results may differ from the reference program's by a relative error of at most 0.019.
Values may be sent and summed in bfloat16 or wider, within the bound.
No kernel may reach another device: no remote copies, remote signals or barrier semaphores. Data moves between devices by JAX's collectives and lax.ppermute only.
A program may use at most 64 MiB of HBM per device.

```python
import jax
import jax.numpy as jnp
from jax import lax

D = 2048
H = 16
FFW = 8192
S = 256
PAGE = 128
MAXP = 8
REQ_DEV = 1
REQ_R = 32
POOL_DEV = 8
POOL = 256
N_ROW = 8


def draw_kv_pool(key, part):
    first = jax.random.fold_in(key, 0)
    shape = (2, 2, POOL, PAGE, D)
    base = jax.random.normal(first, shape, jnp.float32)
    return jnp.clip(base, -240.0, 240.0).astype(jnp.bfloat16)


def draw_page_table(key, part):
    blocks = 2 * (REQ_R // REQ_DEV)
    keys = jax.random.split(jax.random.fold_in(key, 7), blocks)
    perms = jax.vmap(lambda single: jax.random.permutation(single, POOL_DEV))(keys)
    return perms.astype(jnp.int32).reshape(2, REQ_R, MAXP)


def draw_lengths(key, part):
    drawn = jax.random.randint(jax.random.fold_in(key, 11), (2, REQ_R), 1, MAXP * PAGE + 1, jnp.int32)
    return drawn.at[0, 0].set(MAXP * PAGE)


def with_ends(values, own_key, smallest, top_value):
    shape = values.shape
    spot = [jax.random.randint(jax.random.fold_in(own_key, axis), (), 0, shape[axis]) for axis in range(len(shape))]
    values = values.at[tuple(spot)].set(smallest)
    longest = shape.index(max(shape))
    spot[longest] = (spot[longest] + 1) % shape[longest]
    return values.at[tuple(spot)].set(top_value)


def shard_levels(own_key, shape, cuts, smallest, top_value):
    factor_of = 1.0
    for axis_at, blocks in cuts:
        heights = jax.random.uniform(jax.random.fold_in(jax.random.fold_in(own_key, 6), axis_at), (blocks,), jnp.float32, smallest / len(cuts), top_value / len(cuts))
        factor_of = factor_of * jnp.repeat(jnp.exp(heights), shape[axis_at] // blocks).reshape((-1,) + (1,) * (len(shape) - 1 - axis_at))
    return factor_of


def gaussian(own_key, dims, scale, limit, pieces=(), kind=jnp.bfloat16):
    entries = scale * jax.random.normal(own_key, dims, jnp.float32)
    if pieces:
        entries = entries * shard_levels(own_key, dims, pieces, -0.22, 0.18)
    return jnp.clip(entries, -limit, limit).astype(kind)


def setup_inputs(seed: int = 0) -> dict:
    key_list = jax.random.split(jax.random.key(seed), 12)
    return {
        "tokens": gaussian(key_list[0], (2, REQ_R, S, D), 1.0, 6.0, ((0, 2), (1, 32), (3, 8))),
        "w_qkv": gaussian(key_list[1], (D, 3, D), D ** -0.5, 0.125, ((0, 32), (2, 8))),
        "w_out": gaussian(key_list[2], (D, D), D ** -0.5, 0.125, ((0, 8), (1, 32))),
        "w_up": gaussian(key_list[3], (D, FFW), D ** -0.5, 0.125, ((0, 32), (1, 8))),
        "w_down": gaussian(key_list[4], (FFW, D), FFW ** -0.5, 0.0625, ((0, 8), (1, 32))),
        "ln1_gain": jnp.clip(1.0 + 0.15 * jax.random.normal(key_list[5], (D,), jnp.float32), 0.25, 1.75),
        "ln2_gain": jnp.clip(1.0 + 0.15 * jax.random.normal(key_list[6], (D,), jnp.float32), 0.25, 1.75),
        "kv_pool": draw_kv_pool(jax.random.fold_in(key_list[11], 71), 0),
        "page_table": draw_page_table(jax.random.fold_in(key_list[11], 71), 0),
        "lengths": draw_lengths(jax.random.fold_in(key_list[11], 71), 0),
        "moved": with_ends((jax.random.randint(key_list[10], (REQ_R,), 0, 3) < 1).astype(jnp.int32), jax.random.fold_in(key_list[10], 1), 0, 1),
    }


def normalize(values, gain):
    mean = lax.optimization_barrier(jnp.mean(values, axis=-1, keepdims=True))
    centred = values - mean
    spread = lax.optimization_barrier(jnp.mean(centred * centred, axis=-1, keepdims=True))
    return centred * lax.rsqrt(spread + 1e-05) * gain

def attend(query, new_keys, new_values, cache_keys, cache_values, length, slopes):
    seq = query.shape[0]
    heads = query.shape[1]
    head_width = query.shape[2]
    cache_len = cache_keys.shape[0]
    keys = jnp.concatenate([cache_keys, new_keys], axis=0).reshape(-1, heads, head_width)
    values = jnp.concatenate([cache_values, new_values], axis=0).reshape(-1, heads, head_width)
    scores = jnp.einsum('shd,khd->hsk', query.astype(jnp.float32), keys.astype(jnp.float32))
    scores = scores * (1.0 / jnp.sqrt(jnp.float32(head_width)))
    steps = jnp.arange(seq, dtype=jnp.int32)
    cache_pos = jnp.arange(cache_len, dtype=jnp.int32)
    query_pos = length + steps
    key_pos = jnp.concatenate([cache_pos, length + steps])
    cache_ok = jnp.broadcast_to((cache_pos < length)[None, :], (seq, cache_len))
    new_ok = steps[None, :] <= steps[:, None]
    allowed = jnp.concatenate([cache_ok, new_ok], axis=1)
    distance = (query_pos[:, None] - key_pos[None, :]).astype(jnp.float32)
    scores = scores - slopes[:, None, None] * distance[None, :, :]
    masked = jnp.where(allowed[None], scores, -1e+30)
    top = lax.optimization_barrier(jnp.max(masked, axis=-1, keepdims=True))
    weights = jnp.where(allowed[None], jnp.exp(masked - top), 0.0)
    total = lax.optimization_barrier(jnp.sum(weights, axis=-1))
    rounded = weights.astype(jnp.bfloat16).astype(jnp.float32)
    summed = jnp.einsum('hsk,khd->shd', rounded, values.astype(jnp.float32))
    result = summed / jnp.transpose(total)[:, :, None]
    return result.reshape(seq, heads * head_width).astype(jnp.bfloat16)

def grouped_sum(left, right, groups):
    seq = left.shape[0]
    inner = left.shape[1] // groups
    parts = jnp.einsum('sgf,gfd->gsd', left.reshape(seq, groups, inner).astype(jnp.float32), right.reshape(groups, inner, right.shape[1]).astype(jnp.float32))
    rounded = lax.optimization_barrier(parts.astype(jnp.bfloat16))
    return lax.optimization_barrier(jnp.sum(rounded.astype(jnp.float32), axis=0))

def reference(tokens, w_qkv, w_out, w_up, w_down, ln1_gain, ln2_gain, kv_pool, page_table, lengths, moved):
    per_rep = tokens.shape[1]
    head_width = D // H
    slopes = 2.0 ** (-8.0 * (jnp.arange(H).astype(jnp.float32) + 1.0) / H)
    qkv_matrix = w_qkv.reshape(D, 3 * D)

    def serve(index):
        replica = index // per_rep
        slot = index % per_rep
        inputs = tokens[replica, slot]
        normed = normalize(inputs.astype(jnp.float32), ln1_gain).astype(jnp.bfloat16)
        qkv = jnp.dot(normed, qkv_matrix, preferred_element_type=jnp.float32).astype(jnp.bfloat16).reshape(S, 3, D)
        home = jnp.where(moved[slot] == 1, 1 - replica, replica).astype(jnp.int32)
        table = page_table[home, slot]
        length = lengths[home, slot]
        pages = (slot // REQ_DEV * POOL_DEV + table).astype(jnp.int32)
        cache_keys = kv_pool[home, 0, pages].reshape(-1, D)
        cache_values = kv_pool[home, 1, pages].reshape(-1, D)
        query = qkv[:, 0].reshape(S, H, head_width)
        attn = attend(query, qkv[:, 1], qkv[:, 2], cache_keys, cache_values, length, slopes)
        mix = grouped_sum(attn, w_out, N_ROW)
        state = (inputs.astype(jnp.float32) + mix).astype(jnp.bfloat16)
        normed2 = normalize(state.astype(jnp.float32), ln2_gain).astype(jnp.bfloat16)
        hidden = jax.nn.gelu(jnp.dot(normed2, w_up, preferred_element_type=jnp.float32), approximate=True).astype(jnp.bfloat16)
        down = grouped_sum(hidden, w_down, N_ROW)
        return (state.astype(jnp.float32) + down).astype(jnp.bfloat16)
    served = lax.map(serve, jnp.arange(2 * per_rep, dtype=jnp.int32))
    return served.reshape(tokens.shape)
```

```python
import jax
import jax.numpy as jnp
from jax import lax
from jax.sharding import PartitionSpec as P

D = 2048
H = 16


def swapped(value, axis, apart):
    return lax.ppermute(value, axis, [(i, i ^ 1 << apart) for i in range(lax.axis_size(axis))])


def normalize(values, gain):
    mean = jnp.mean(values, axis=-1, keepdims=True)
    centred = values - mean
    spread = jnp.mean(centred * centred, axis=-1, keepdims=True)
    return centred * lax.rsqrt(spread + 1e-05) * gain


def attend(query, new_keys, new_values, cache_keys, cache_values, length, slopes):
    seq = query.shape[0]
    heads = query.shape[1]
    head_width = query.shape[2]
    cache_len = cache_keys.shape[0]
    keys = jnp.concatenate([cache_keys, new_keys], axis=0).reshape(-1, heads, head_width)
    values = jnp.concatenate([cache_values, new_values], axis=0).reshape(-1, heads, head_width)
    scores = jnp.einsum("shd,khd->hsk", query, keys, preferred_element_type=jnp.float32)
    scores = scores * (1.0 / jnp.sqrt(jnp.float32(head_width)))
    steps = jnp.arange(seq, dtype=jnp.int32)
    cache_pos = jnp.arange(cache_len, dtype=jnp.int32)
    query_pos = length + steps
    key_pos = jnp.concatenate([cache_pos, length + steps])
    cache_ok = jnp.broadcast_to((cache_pos < length)[None, :], (seq, cache_len))
    new_ok = steps[None, :] <= steps[:, None]
    allowed = jnp.concatenate([cache_ok, new_ok], axis=1)
    distance = (query_pos[:, None] - key_pos[None, :]).astype(jnp.float32)
    scores = scores - slopes[:, None, None] * distance[None, :, :]
    masked = jnp.where(allowed[None], scores, -1e30)
    top = jnp.max(masked, axis=-1, keepdims=True)
    weights = jnp.where(allowed[None], jnp.exp(masked - top), 0.0)
    total = jnp.sum(weights, axis=-1)
    summed = jnp.einsum(
        "hsk,khd->shd", weights.astype(jnp.bfloat16), values, preferred_element_type=jnp.float32
    )
    result = summed / jnp.transpose(total)[:, :, None]
    return result.reshape(seq, heads * head_width).astype(jnp.bfloat16)


def row_gather(value):
    copies = jnp.broadcast_to(value[None], (lax.axis_size("row"),) + value.shape)
    parts = lax.all_to_all(copies, "row", 0, 0, tiled=True)
    return jnp.swapaxes(parts, 0, 1).reshape(value.shape[0], -1)


def row_scatter_sum(partial):
    size = lax.axis_size("row")
    parts = partial.reshape(partial.shape[0], size, -1)
    parts = jnp.swapaxes(parts, 0, 1).astype(jnp.bfloat16)
    parts = lax.all_to_all(parts, "row", 0, 0, tiled=True)
    return jnp.sum(parts.astype(jnp.float32), axis=0)


def times_transposed(left, right):
    return lax.dot_general(left, right, (((1,), (1,)), ((), ())), preferred_element_type=jnp.float32)


def local(
    tokens, w_qkv, w_out, w_up, w_down, ln1_gain, ln2_gain, kv_pool, page_table, lengths, moved
):
    rep_index = lax.axis_index("rep")
    row_index = lax.axis_index("row")
    seq = tokens.shape[2]
    share = tokens.shape[3]
    hidden_share = w_up.shape[1]
    head_width = D // H
    heads = share // head_width
    shard = jnp.concatenate(
        [w_qkv.reshape(w_qkv.shape[0], -1), w_out.T, w_up, w_down.T], axis=1
    )
    weights = lax.all_gather(shard, "col", axis=0, tiled=True)
    cut = [0, 3 * share, 4 * share, 4 * share + hidden_share, 4 * share + 2 * hidden_share]
    all_qkv, all_out, all_up, all_down = [weights[:, a:b] for a, b in zip(cut[:-1], cut[1:])]
    other = swapped(kv_pool, "rep", 0)
    inputs = tokens.reshape(seq, share)
    rows = row_gather(inputs)
    normed = normalize(rows.astype(jnp.float32), ln1_gain).astype(jnp.bfloat16)
    head_ids = (row_index * heads + jnp.arange(heads, dtype=jnp.int32) + 1).astype(jnp.float32)
    slopes = 2.0 ** (-8.0 * head_ids / H)

    def pages_of(store, table):
        return store[table].reshape(-1, store.shape[2])

    flag = moved[0] == 1
    home = jnp.where(flag, 1 - rep_index, rep_index)
    table = page_table[home, 0]
    length = lengths[home, 0]
    cache_keys = jnp.where(flag, pages_of(other[0, 0], table), pages_of(kv_pool[0, 0], table))
    cache_values = jnp.where(flag, pages_of(other[0, 1], table), pages_of(kv_pool[0, 1], table))
    qkv = jnp.dot(normed, all_qkv, preferred_element_type=jnp.float32)
    qkv = qkv.astype(jnp.bfloat16).reshape(seq, 3, share)
    query = qkv[:, 0].reshape(seq, heads, head_width)
    attn = attend(query, qkv[:, 1], qkv[:, 2], cache_keys, cache_values, length, slopes)
    mixed = row_scatter_sum(times_transposed(attn, all_out))
    state_local = (inputs.astype(jnp.float32) + mixed).astype(jnp.bfloat16)
    state = row_gather(state_local)
    normed2 = normalize(state.astype(jnp.float32), ln2_gain).astype(jnp.bfloat16)
    hidden = jax.nn.gelu(
        jnp.dot(normed2, all_up, preferred_element_type=jnp.float32), approximate=True
    ).astype(jnp.bfloat16)
    down = row_scatter_sum(times_transposed(hidden, all_down))
    finished = (state_local.astype(jnp.float32) + down).astype(jnp.bfloat16)
    return finished.reshape(tokens.shape)


def solution(mesh):
    return jax.shard_map(
        local,
        mesh=mesh,
        in_specs=(
            P("rep", "col", None, "row"),
            P("col", None, "row"),
            P("row", "col"),
            P("col", "row"),
            P("row", "col"),
            P(),
            P(),
            P("rep", None, "col", None, "row"),
            P(None, "col", None),
            P(None, "col"),
            P("col"),
        ),
        out_specs=P("rep", "col", None, "row"),
        check_vma=False,
    )
```

```python
import jax
import jax.numpy as jnp
from jax import lax
from jax.experimental import pallas as pl
from jax.experimental.pallas import tpu as pltpu
from jax.sharding import PartitionSpec as P

D = 2048
H = 16


def swapped(value, axis, apart):
    return lax.ppermute(value, axis, [(i, i ^ 1 << apart) for i in range(lax.axis_size(axis))])


def normalize(values, gain):
    mean = jnp.mean(values, axis=-1, keepdims=True)
    centred = values - mean
    spread = jnp.mean(centred * centred, axis=-1, keepdims=True)
    return centred * lax.rsqrt(spread + 1e-05) * gain


def attend_kernel(scalars, slopes, normed, weights, out_weights, keys, values, mixed, total, attn):
    step = pl.program_id(0)
    product = jnp.dot(normed[...], weights[...], preferred_element_type=jnp.float32)

    @pl.when(step == 0)
    def _():
        total[...] = product

    @pl.when(step > 0)
    def _():
        total[...] += product

    @pl.when(step == pl.num_programs(0) - 1)
    def _():
        length = scalars[0]
        seq = normed.shape[0]
        cached = keys.shape[0]
        share = keys.shape[1]
        head_width = D // H
        scale = jnp.float32(head_width) ** -0.5
        cache_pos = lax.broadcasted_iota(jnp.int32, (1, cached), 1)
        cache_ok = cache_pos < length
        cache_off = (cache_pos - length).astype(jnp.float32)
        new_pos = lax.broadcasted_iota(jnp.int32, (seq, seq), 1)
        new_ok = new_pos <= lax.broadcasted_iota(jnp.int32, (seq, seq), 0)
        new_off = lax.broadcasted_iota(jnp.int32, (1, seq), 1).astype(jnp.float32)
        for head in range(share // head_width):
            lanes = slice(head * head_width, (head + 1) * head_width)

            def part(index):
                start = index * share + head * head_width
                return total[:, start : start + head_width].astype(jnp.bfloat16)

            query, new_key, new_value = part(0), part(1), part(2)
            slope = slopes[head]
            cache_score = times_transposed(query, keys[:, lanes]) * scale
            cache_score = jnp.where(cache_ok, cache_score + slope * cache_off, -1e30)
            new_score = times_transposed(query, new_key) * scale
            new_score = jnp.where(new_ok, new_score + slope * new_off, -1e30)
            top = jnp.maximum(
                jnp.max(cache_score, axis=1, keepdims=True),
                jnp.max(new_score, axis=1, keepdims=True),
            )
            cache_weight = jnp.exp(cache_score - top)
            new_weight = jnp.exp(new_score - top)
            whole = jnp.sum(cache_weight, axis=1, keepdims=True) + jnp.sum(
                new_weight, axis=1, keepdims=True
            )
            summed = jnp.dot(
                cache_weight.astype(jnp.bfloat16), values[:, lanes], preferred_element_type=jnp.float32
            ) + jnp.dot(new_weight.astype(jnp.bfloat16), new_value, preferred_element_type=jnp.float32)
            attn[:, lanes] = (summed / whole).astype(jnp.bfloat16)
        for row in range(mixed.shape[0]):
            rows = slice(row * share, (row + 1) * share)
            mixed[row] = times_transposed(attn[...], out_weights[rows, :]).astype(jnp.bfloat16)


def attend(normed, weights, keys, values, length, slopes, rows):
    seq, width = normed.shape
    share = keys.shape[1]
    steps = 4
    deep = width // steps
    return pl.pallas_call(
        attend_kernel,
        out_shape=jax.ShapeDtypeStruct((rows, seq, share), jnp.bfloat16),
        grid_spec=pltpu.PrefetchScalarGridSpec(
            num_scalar_prefetch=2,
            grid=(steps,),
            in_specs=[
                pl.BlockSpec((seq, deep), lambda k, *_: (0, k)),
                pl.BlockSpec((deep, 3 * share), lambda k, *_: (k, 0)),
                pl.BlockSpec((width, share), lambda k, *_: (0, 3)),
                pl.BlockSpec(keys.shape, lambda k, *_: (0, 0)),
                pl.BlockSpec(values.shape, lambda k, *_: (0, 0)),
            ],
            out_specs=pl.BlockSpec((rows, seq, share), lambda k, *_: (0, 0, 0)),
            scratch_shapes=[
                pltpu.VMEM((seq, 3 * share), jnp.float32),
                pltpu.VMEM((seq, share), jnp.bfloat16),
            ],
        ),
        compiler_params=pltpu.CompilerParams(vmem_limit_bytes=48 << 20),
    )(length.reshape(1), slopes, normed, weights, weights, keys, values)


def feed_kernel(state, gain, up_weights, down_weights, down, normed, total):
    step = pl.program_id(0)
    rows, seq, share = state.shape
    width = rows * share

    @pl.when(step == 0)
    def _():
        pieces = [state[row].astype(jnp.float32) for row in range(rows)]
        mean = sum(jnp.sum(piece, axis=1, keepdims=True) for piece in pieces) / width
        centred = [piece - mean for piece in pieces]
        spread = sum(jnp.sum(piece * piece, axis=1, keepdims=True) for piece in centred) / width
        factor = lax.rsqrt(spread + 1e-05)
        for row in range(rows):
            lanes = slice(row * share, (row + 1) * share)
            normed[:, lanes] = (centred[row] * factor * gain[:, lanes]).astype(jnp.bfloat16)

    hidden = jax.nn.gelu(
        jnp.dot(normed[...], up_weights[...], preferred_element_type=jnp.float32), approximate=True
    ).astype(jnp.bfloat16)
    product = times_transposed(hidden, down_weights[...])

    @pl.when(step == 0)
    def _():
        total[...] = product

    @pl.when(step > 0)
    def _():
        total[...] += product

    @pl.when(step == pl.num_programs(0) - 1)
    def _():
        for row in range(rows):
            down[row] = total[:, row * share : (row + 1) * share].astype(jnp.bfloat16)


def feed(state, gain, weights, hidden_share):
    rows, seq, share = state.shape
    width = rows * share
    steps = 4
    each = hidden_share // steps
    up_from = 4 * share // each
    return pl.pallas_call(
        feed_kernel,
        out_shape=jax.ShapeDtypeStruct(state.shape, jnp.bfloat16),
        grid=(steps,),
        in_specs=[
            pl.BlockSpec(state.shape, lambda k: (0, 0, 0)),
            pl.BlockSpec((1, width), lambda k: (0, 0)),
            pl.BlockSpec((width, each), lambda k: (0, up_from + k)),
            pl.BlockSpec((width, each), lambda k: (0, up_from + steps + k)),
        ],
        out_specs=pl.BlockSpec(state.shape, lambda k: (0, 0, 0)),
        scratch_shapes=[
            pltpu.VMEM((seq, width), jnp.bfloat16),
            pltpu.VMEM((seq, width), jnp.float32),
        ],
        compiler_params=pltpu.CompilerParams(vmem_limit_bytes=48 << 20),
    )(state, gain.reshape(1, width), weights, weights)


def row_gather(value):
    copies = jnp.broadcast_to(value[None], (lax.axis_size("row"),) + value.shape)
    return lax.all_to_all(copies, "row", 0, 0, tiled=True)


def row_scatter_sum(parts):
    parts = lax.all_to_all(parts, "row", 0, 0, tiled=True)
    return jnp.sum(parts.astype(jnp.float32), axis=0)


def times_transposed(left, right):
    return lax.dot_general(left, right, (((1,), (1,)), ((), ())), preferred_element_type=jnp.float32)


def local(
    tokens, w_qkv, w_out, w_up, w_down, ln1_gain, ln2_gain, kv_pool, page_table, lengths, moved
):
    rep_index = lax.axis_index("rep")
    row_index = lax.axis_index("row")
    seq = tokens.shape[2]
    share = tokens.shape[3]
    hidden_share = w_up.shape[1]
    head_width = D // H
    heads = share // head_width
    shard = jnp.concatenate(
        [w_qkv.reshape(w_qkv.shape[0], -1), w_out.T, w_up, w_down.T], axis=1
    )
    weights = lax.all_gather(shard, "col", axis=0, tiled=True)
    other = swapped(kv_pool, "rep", 0)
    inputs = tokens.reshape(seq, share)
    rows = jnp.swapaxes(row_gather(inputs), 0, 1).reshape(seq, D)
    normed = normalize(rows.astype(jnp.float32), ln1_gain).astype(jnp.bfloat16)
    head_ids = (row_index * heads + jnp.arange(heads, dtype=jnp.int32) + 1).astype(jnp.float32)
    slopes = 2.0 ** (-8.0 * head_ids / H)

    def pages_of(store, table):
        return store[table].reshape(-1, store.shape[2])

    flag = moved[0] == 1
    home = jnp.where(flag, 1 - rep_index, rep_index)
    table = page_table[home, 0]
    length = lengths[home, 0]
    cache_keys = jnp.where(flag, pages_of(other[0, 0], table), pages_of(kv_pool[0, 0], table))
    cache_values = jnp.where(flag, pages_of(other[0, 1], table), pages_of(kv_pool[0, 1], table))
    partial_mix = attend(
        normed, weights, cache_keys, cache_values, length, slopes, lax.axis_size("row")
    )
    mixed = row_scatter_sum(partial_mix)
    state_local = (inputs.astype(jnp.float32) + mixed).astype(jnp.bfloat16)
    down = row_scatter_sum(feed(row_gather(state_local), ln2_gain, weights, hidden_share))
    finished = (state_local.astype(jnp.float32) + down).astype(jnp.bfloat16)
    return finished.reshape(tokens.shape)


def solution(mesh):
    return jax.shard_map(
        local,
        mesh=mesh,
        in_specs=(
            P("rep", "col", None, "row"),
            P("col", None, "row"),
            P("row", "col"),
            P("col", "row"),
            P("row", "col"),
            P(),
            P(),
            P("rep", None, "col", None, "row"),
            P(None, "col", None),
            P(None, "col"),
            P("col"),
        ),
        out_specs=P("rep", "col", None, "row"),
        check_vma=False,
    )
```

```python
import jax
import jax.numpy as jnp
from jax import lax
from jax.experimental import pallas as pl
from jax.experimental.pallas import tpu as pltpu
from jax.sharding import Mesh
from jax.sharding import PartitionSpec as P

D = 2048
H = 16


def swapped(value, axis, apart):
    return lax.ppermute(value, axis, [(i, i ^ 1 << apart) for i in range(lax.axis_size(axis))])


def normalize(values, gain):
    mean = jnp.mean(values, axis=-1, keepdims=True)
    centred = values - mean
    spread = jnp.mean(centred * centred, axis=-1, keepdims=True)
    return centred * lax.rsqrt(spread + 1e-05) * gain


def attend_kernel(scalars, slopes, normed, weights, keys, values, copies, total, attn):
    step = pl.program_id(0)
    product = jnp.dot(normed[...], weights[...], preferred_element_type=jnp.float32)

    @pl.when(step == 0)
    def _():
        total[...] = product

    @pl.when(step > 0)
    def _():
        total[...] += product

    @pl.when(step == pl.num_programs(0) - 1)
    def _():
        length = scalars[0]
        seq = normed.shape[0]
        cached = keys.shape[0]
        share = keys.shape[1]
        head_width = D // H
        scale = jnp.float32(head_width) ** -0.5
        cache_pos = lax.broadcasted_iota(jnp.int32, (1, cached), 1)
        cache_ok = cache_pos < length
        cache_off = (cache_pos - length).astype(jnp.float32)
        new_pos = lax.broadcasted_iota(jnp.int32, (seq, seq), 1)
        new_ok = new_pos <= lax.broadcasted_iota(jnp.int32, (seq, seq), 0)
        new_off = lax.broadcasted_iota(jnp.int32, (1, seq), 1).astype(jnp.float32)
        for head in range(share // head_width):
            lanes = slice(head * head_width, (head + 1) * head_width)

            def part(index):
                start = index * share + head * head_width
                return total[:, start : start + head_width].astype(jnp.bfloat16)

            query, new_key, new_value = part(0), part(1), part(2)
            slope = slopes[head]
            cache_score = times_transposed(query, keys[:, lanes]) * scale
            cache_score = jnp.where(cache_ok, cache_score + slope * cache_off, -1e30)
            new_score = times_transposed(query, new_key) * scale
            new_score = jnp.where(new_ok, new_score + slope * new_off, -1e30)
            top = jnp.maximum(
                jnp.max(cache_score, axis=1, keepdims=True),
                jnp.max(new_score, axis=1, keepdims=True),
            )
            cache_weight = jnp.exp(cache_score - top)
            new_weight = jnp.exp(new_score - top)
            whole = jnp.sum(cache_weight, axis=1, keepdims=True) + jnp.sum(
                new_weight, axis=1, keepdims=True
            )
            summed = jnp.dot(
                cache_weight.astype(jnp.bfloat16), values[:, lanes], preferred_element_type=jnp.float32
            ) + jnp.dot(new_weight.astype(jnp.bfloat16), new_value, preferred_element_type=jnp.float32)
            attn[:, lanes] = (summed / whole).astype(jnp.bfloat16)
        for row in range(copies.shape[0]):
            copies[row] = attn[...]


def attend(normed, weights, keys, values, length, slopes, rows):
    seq, width = normed.shape
    share = keys.shape[1]
    steps = 4
    deep = width // steps
    return pl.pallas_call(
        attend_kernel,
        out_shape=jax.ShapeDtypeStruct((rows, seq, share), jnp.bfloat16),
        grid_spec=pltpu.PrefetchScalarGridSpec(
            num_scalar_prefetch=2,
            grid=(steps,),
            in_specs=[
                pl.BlockSpec((seq, deep), lambda k, *_: (0, k)),
                pl.BlockSpec((deep, 3 * share), lambda k, *_: (k, 0)),
                pl.BlockSpec(keys.shape, lambda k, *_: (0, 0)),
                pl.BlockSpec(values.shape, lambda k, *_: (0, 0)),
            ],
            out_specs=pl.BlockSpec((rows, seq, share), lambda k, *_: (0, 0, 0)),
            scratch_shapes=[
                pltpu.VMEM((seq, 3 * share), jnp.float32),
                pltpu.VMEM((seq, share), jnp.bfloat16),
            ],
        ),
        compiler_params=pltpu.CompilerParams(vmem_limit_bytes=48 << 20),
    )(length.reshape(1), slopes, normed, weights, keys, values)


def feed_kernel(place, attns, tokens, gain, near, far, gathered, down, state_local,
                out_weights, feed_weights, wide, state, hidden, sems):
    rows, seq, share = attns.shape
    width = rows * share
    hidden_share = feed_weights.shape[2]
    chips = near.shape[1]
    first = 3 * share
    copies = []

    def copy(source, target):
        copies.append(pltpu.make_async_copy(source, target, sems.at[len(copies)]))
        copies[-1].start()

    for row in range(rows):
        lanes = pl.ds(row * share, share)
        copy(near.at[row], out_weights.at[:, place[0], :, lanes])
        copy(far.at[row], out_weights.at[:, 1 - place[0], :, lanes])
    for part in range(2):
        copy(gathered.at[:, pl.ds(first + part * hidden_share, hidden_share)], feed_weights.at[part])
    for row in range(rows):
        wide[:, row * share : (row + 1) * share] = attns[row]
    for item in copies[: 2 * rows]:
        item.wait()
    each = chips // rows
    for row in range(rows):
        block = out_weights[row * each : (row + 1) * each].reshape(share, width)
        mixed = times_transposed(wide[...], block)
        state[row] = (tokens[row].astype(jnp.float32) + mixed).astype(jnp.bfloat16)
    state_local[...] = state[place[1]]
    pieces = [state[row].astype(jnp.float32) for row in range(rows)]
    mean = sum(jnp.sum(piece, axis=1, keepdims=True) for piece in pieces) / width
    centred = [piece - mean for piece in pieces]
    spread = sum(jnp.sum(piece * piece, axis=1, keepdims=True) for piece in centred) / width
    factor = lax.rsqrt(spread + 1e-05)
    for row in range(rows):
        lanes = slice(row * share, (row + 1) * share)
        wide[:, lanes] = (centred[row] * factor * gain[:, lanes]).astype(jnp.bfloat16)
    copies[2 * rows].wait()
    for part in range(4):
        lanes = slice(part * hidden_share // 4, (part + 1) * hidden_share // 4)
        up = jnp.dot(wide[...], feed_weights[0, :, lanes], preferred_element_type=jnp.float32)
        hidden[:, lanes] = jax.nn.gelu(up, approximate=True).astype(jnp.bfloat16)
    copies[2 * rows + 1].wait()
    for row in range(rows):
        lanes = slice(row * share, (row + 1) * share)
        down[row] = times_transposed(hidden[...], feed_weights[1, lanes, :]).astype(jnp.bfloat16)


def feed(place, attns, tokens, gain, near, far, gathered, hidden_share):
    rows, seq, share = attns.shape
    width = rows * share
    chips = near.shape[1]
    return pl.pallas_call(
        feed_kernel,
        out_shape=(
            jax.ShapeDtypeStruct(attns.shape, jnp.bfloat16),
            jax.ShapeDtypeStruct((seq, share), jnp.bfloat16),
        ),
        grid_spec=pltpu.PrefetchScalarGridSpec(
            num_scalar_prefetch=1,
            grid=(1,),
            in_specs=[
                pl.BlockSpec(attns.shape, lambda *_: (0, 0, 0)),
                pl.BlockSpec(tokens.shape, lambda *_: (0, 0, 0)),
                pl.BlockSpec((1, width), lambda *_: (0, 0)),
                pl.BlockSpec(memory_space=pl.ANY),
                pl.BlockSpec(memory_space=pl.ANY),
                pl.BlockSpec(memory_space=pl.ANY),
            ],
            out_specs=(
                pl.BlockSpec(attns.shape, lambda *_: (0, 0, 0)),
                pl.BlockSpec((seq, share), lambda *_: (0, 0)),
            ),
            scratch_shapes=[
                pltpu.VMEM((chips, 2, width // chips // 2, width), jnp.bfloat16),
                pltpu.VMEM((2, width, hidden_share), jnp.bfloat16),
                pltpu.VMEM((seq, width), jnp.bfloat16),
                pltpu.VMEM(attns.shape, jnp.bfloat16),
                pltpu.VMEM((seq, hidden_share), jnp.bfloat16),
                pltpu.SemaphoreType.DMA((2 * rows + 2,)),
            ],
        ),
        compiler_params=pltpu.CompilerParams(vmem_limit_bytes=48 << 20),
    )(place, attns, tokens, gain.reshape(1, width), near, far, gathered)


def row_exchange(parts):
    return lax.all_to_all(parts, "row", 0, 0, tiled=True)


def row_gather(value):
    return row_exchange(jnp.broadcast_to(value[None], (lax.axis_size("row"),) + value.shape))


def row_scatter_sum(parts):
    parts = row_exchange(parts)
    return jnp.sum(parts.astype(jnp.float32), axis=0)


def times_transposed(left, right):
    return lax.dot_general(left, right, (((1,), (1,)), ((), ())), preferred_element_type=jnp.float32)


def local(
    tokens, w_qkv, w_out, w_up, w_down, ln1_gain, ln2_gain, kv_pool, page_table, lengths, moved
):
    rep_index = lax.axis_index("rep")
    row_index = lax.axis_index("row")
    seq = tokens.shape[2]
    share = tokens.shape[3]
    hidden_share = w_up.shape[1]
    head_width = D // H
    heads = share // head_width
    inputs = tokens.reshape(seq, share)
    spread_tokens = row_gather(inputs)
    shard = jnp.concatenate([w_qkv.reshape(w_qkv.shape[0], -1), w_up, w_down.T], axis=1)
    weights = lax.all_gather(shard, ("z", "core"), axis=0, tiled=True)
    other = swapped(kv_pool, "rep", 0)
    out_block = lax.all_gather(w_out.T, "z", axis=0, tiled=False)
    out_block, spread_tokens, other = lax.optimization_barrier((out_block, spread_tokens, other))
    near = row_gather(out_block)
    rows = jnp.swapaxes(spread_tokens, 0, 1).reshape(seq, D)
    normed = normalize(rows.astype(jnp.float32), ln1_gain).astype(jnp.bfloat16)
    head_ids = (row_index * heads + jnp.arange(heads, dtype=jnp.int32) + 1).astype(jnp.float32)
    slopes = 2.0 ** (-8.0 * head_ids / H)

    def pages_of(store, table):
        return store[table].reshape(-1, store.shape[2])

    flag = moved[0] == 1
    home = jnp.where(flag, 1 - rep_index, rep_index)
    table = page_table[home, 0]
    length = lengths[home, 0]
    cache_keys = jnp.where(flag, pages_of(other[0, 0], table), pages_of(kv_pool[0, 0], table))
    cache_values = jnp.where(flag, pages_of(other[0, 1], table), pages_of(kv_pool[0, 1], table))
    attn_copies = attend(
        normed, weights, cache_keys, cache_values, length, slopes, lax.axis_size("row")
    )
    attns = row_exchange(attn_copies)
    near, _ = lax.optimization_barrier((near, attn_copies))
    far = swapped(near, "core", 0)
    place = jnp.stack([lax.axis_index("core"), row_index]).astype(jnp.int32)
    partial_down, state_local = feed(
        place, attns, spread_tokens, ln2_gain, near, far, weights, hidden_share
    )
    down = row_scatter_sum(partial_down)
    finished = (state_local.astype(jnp.float32) + down).astype(jnp.bfloat16)
    return finished.reshape(tokens.shape)


def solution(mesh):
    reps, rows, cols = mesh.devices.shape
    mesh = Mesh(mesh.devices.reshape(reps, rows, cols // 2, 2), ("rep", "row", "z", "core"))
    col = ("z", "core")
    return jax.shard_map(
        local,
        mesh=mesh,
        in_specs=(
            P("rep", col, None, "row"),
            P(col, None, "row"),
            P("row", col),
            P(col, "row"),
            P("row", col),
            P(),
            P(),
            P("rep", None, col, None, "row"),
            P(None, col, None),
            P(None, col),
            P(col),
        ),
        out_specs=P("rep", col, None, "row"),
        check_vma=False,
    )
```

```python
import math

import jax
import jax.numpy as jnp
from jax import lax
from jax.experimental import pallas as pl
from jax.experimental.pallas import tpu as pltpu
from jax.sharding import Mesh
from jax.sharding import PartitionSpec as P

D = 2048
H = 16
GROUPS = 4


def swapped(value, axis, apart):
    return lax.ppermute(value, axis, [(i, i ^ 1 << apart) for i in range(lax.axis_size(axis))])


def normalize(values, gain):
    mean = jnp.mean(values, axis=-1, keepdims=True)
    centred = values - mean
    spread = jnp.mean(centred * centred, axis=-1, keepdims=True)
    return centred * lax.rsqrt(spread + 1e-05) * gain


def attend_kernel(scalars, slopes, normed, weights, keys, values, copies, total, attn):
    step = pl.program_id(0)
    product = jnp.dot(normed[...], weights[...], preferred_element_type=jnp.float32)

    @pl.when(step == 0)
    def _():
        total[...] = product

    @pl.when(step > 0)
    def _():
        total[...] += product

    @pl.when(step == pl.num_programs(0) - 1)
    def _():
        length = scalars[0]
        seq = normed.shape[0]
        cached = keys.shape[0]
        share = keys.shape[1]
        head_width = D // H
        fold = jnp.float32(math.log2(math.e))
        scale = fold * jnp.float32(head_width) ** -0.5
        cache_pos = lax.broadcasted_iota(jnp.int32, (1, cached), 1)
        cache_ok = cache_pos < length
        cache_off = (cache_pos - length).astype(jnp.float32)
        new_pos = lax.broadcasted_iota(jnp.int32, (seq, seq), 1)
        new_ok = new_pos <= lax.broadcasted_iota(jnp.int32, (seq, seq), 0)
        new_off = lax.broadcasted_iota(jnp.int32, (1, seq), 1).astype(jnp.float32)
        for head in range(share // head_width):
            lanes = slice(head * head_width, (head + 1) * head_width)

            def part(index):
                start = index * share + head * head_width
                return total[:, start : start + head_width].astype(jnp.bfloat16)

            query, new_key, new_value = part(0), part(1), part(2)
            slope = fold * slopes[head]
            cache_bias = jnp.where(cache_ok, slope * cache_off, -1e30)
            cache_score = times_transposed(query, keys[:, lanes]) * scale + cache_bias
            new_score = times_transposed(query, new_key) * scale + slope * new_off
            new_score = jnp.where(new_ok, new_score, -1e30)
            top = jnp.maximum(
                jnp.max(cache_score, axis=1, keepdims=True),
                jnp.max(new_score, axis=1, keepdims=True),
            )
            cache_weight = jnp.exp2(cache_score - top)
            new_weight = jnp.exp2(new_score - top)
            whole = jnp.sum(cache_weight, axis=1, keepdims=True) + jnp.sum(
                new_weight, axis=1, keepdims=True
            )
            summed = jnp.dot(
                cache_weight.astype(jnp.bfloat16), values[:, lanes], preferred_element_type=jnp.float32
            ) + jnp.dot(new_weight.astype(jnp.bfloat16), new_value, preferred_element_type=jnp.float32)
            attn[:, lanes] = (summed / whole).astype(jnp.bfloat16)
        for row in range(copies.shape[0]):
            copies[row] = attn[...]


def attend(normed, weights, keys, values, length, slopes, rows):
    seq, width = normed.shape
    share = keys.shape[1]
    steps = 2
    deep = width // steps
    return pl.pallas_call(
        attend_kernel,
        out_shape=jax.ShapeDtypeStruct((rows, seq, share), jnp.bfloat16),
        grid_spec=pltpu.PrefetchScalarGridSpec(
            num_scalar_prefetch=2,
            grid=(steps,),
            in_specs=[
                pl.BlockSpec((seq, deep), lambda k, *_: (0, k)),
                pl.BlockSpec((deep, 3 * share), lambda k, *_: (k, 0)),
                pl.BlockSpec(keys.shape, lambda k, *_: (0, 0)),
                pl.BlockSpec(values.shape, lambda k, *_: (0, 0)),
            ],
            out_specs=pl.BlockSpec((rows, seq, share), lambda k, *_: (0, 0, 0)),
            scratch_shapes=[
                pltpu.VMEM((seq, 3 * share), jnp.float32),
                pltpu.VMEM((seq, share), jnp.bfloat16),
            ],
        ),
        compiler_params=pltpu.CompilerParams(vmem_limit_bytes=48 << 20),
    )(length.reshape(1), slopes, normed, weights, keys, values)


def feed_kernel(place, attns, tokens, gain, near, far, gathered, down, state_local,
                out_weights, feed_weights, wide, state, hidden, sems):
    rows, seq, share = attns.shape
    width = rows * share
    hidden_share = feed_weights.shape[2]
    chips = near.shape[1]
    first = 3 * share
    copies = []

    def copy(source, target):
        copies.append(pltpu.make_async_copy(source, target, sems.at[len(copies)]))
        copies[-1].start()

    span = chips // GROUPS
    for group in range(GROUPS):
        picked = pl.ds(group * span, span)
        for row in range(rows):
            lanes = pl.ds(row * share, share)
            copy(near.at[row, picked], out_weights.at[picked, place[0], :, lanes])
            copy(far.at[row, picked], out_weights.at[picked, 1 - place[0], :, lanes])
    for part in range(2):
        copy(gathered.at[:, pl.ds(first + part * hidden_share, hidden_share)], feed_weights.at[part])
    for row in range(rows):
        wide[:, row * share : (row + 1) * share] = attns[row]
    each = chips // rows
    for row in range(rows):
        if row % (rows // GROUPS) == 0:
            group = row // (rows // GROUPS)
            for item in copies[2 * rows * group : 2 * rows * (group + 1)]:
                item.wait()
        block = out_weights[row * each : (row + 1) * each].reshape(share, width)
        mixed = times_transposed(wide[...], block)
        state[row] = (tokens[row].astype(jnp.float32) + mixed).astype(jnp.bfloat16)
    state_local[...] = state[place[1]]
    pieces = [state[row].astype(jnp.float32) for row in range(rows)]
    mean = sum(jnp.sum(piece, axis=1, keepdims=True) for piece in pieces) / width
    centred = [piece - mean for piece in pieces]
    spread = sum(jnp.sum(piece * piece, axis=1, keepdims=True) for piece in centred) / width
    factor = lax.rsqrt(spread + 1e-05)
    for row in range(rows):
        lanes = slice(row * share, (row + 1) * share)
        wide[:, lanes] = (centred[row] * factor * gain[:, lanes]).astype(jnp.bfloat16)
    copies[-2].wait()
    for part in range(4):
        lanes = slice(part * hidden_share // 4, (part + 1) * hidden_share // 4)
        up = jnp.dot(wide[...], feed_weights[0, :, lanes], preferred_element_type=jnp.float32)
        hidden[:, lanes] = jax.nn.gelu(up, approximate=True).astype(jnp.bfloat16)
    copies[-1].wait()
    for row in range(rows):
        lanes = slice(row * share, (row + 1) * share)
        down[row] = times_transposed(hidden[...], feed_weights[1, lanes, :]).astype(jnp.bfloat16)


def feed(place, attns, tokens, gain, near, far, gathered, hidden_share):
    rows, seq, share = attns.shape
    width = rows * share
    chips = near.shape[1]
    return pl.pallas_call(
        feed_kernel,
        out_shape=(
            jax.ShapeDtypeStruct(attns.shape, jnp.bfloat16),
            jax.ShapeDtypeStruct((seq, share), jnp.bfloat16),
        ),
        grid_spec=pltpu.PrefetchScalarGridSpec(
            num_scalar_prefetch=1,
            grid=(1,),
            in_specs=[
                pl.BlockSpec(attns.shape, lambda *_: (0, 0, 0)),
                pl.BlockSpec(tokens.shape, lambda *_: (0, 0, 0)),
                pl.BlockSpec((1, width), lambda *_: (0, 0)),
                pl.BlockSpec(memory_space=pl.ANY),
                pl.BlockSpec(memory_space=pl.ANY),
                pl.BlockSpec(memory_space=pl.ANY),
            ],
            out_specs=(
                pl.BlockSpec(attns.shape, lambda *_: (0, 0, 0)),
                pl.BlockSpec((seq, share), lambda *_: (0, 0)),
            ),
            scratch_shapes=[
                pltpu.VMEM((chips, 2, width // chips // 2, width), jnp.bfloat16),
                pltpu.VMEM((2, width, hidden_share), jnp.bfloat16),
                pltpu.VMEM((seq, width), jnp.bfloat16),
                pltpu.VMEM(attns.shape, jnp.bfloat16),
                pltpu.VMEM((seq, hidden_share), jnp.bfloat16),
                pltpu.SemaphoreType.DMA((2 * rows * GROUPS + 2,)),
            ],
        ),
        compiler_params=pltpu.CompilerParams(vmem_limit_bytes=48 << 20),
    )(place, attns, tokens, gain.reshape(1, width), near, far, gathered)


def pack_kernel(qkv, up, down, shard):
    start = 0
    for source in [qkv.at[part] for part in range(qkv.shape[0])] + [up, down]:
        shard[:, start : start + source.shape[1]] = source[...]
        start += source.shape[1]


def pack(qkv, up, down):
    parts, rows, share = qkv.shape
    width = parts * share + up.shape[1] + down.shape[1]
    return pl.pallas_call(
        pack_kernel,
        out_shape=jax.ShapeDtypeStruct((rows, width), jnp.bfloat16),
    )(qkv, up, down)


def row_exchange(parts):
    return lax.all_to_all(parts, "row", 0, 0, tiled=True)


def row_gather(value):
    return row_exchange(jnp.broadcast_to(value[None], (lax.axis_size("row"),) + value.shape))


def row_scatter_sum(parts):
    parts = row_exchange(parts)
    return jnp.sum(parts.astype(jnp.float32), axis=0)


def times_transposed(left, right):
    return lax.dot_general(left, right, (((1,), (1,)), ((), ())), preferred_element_type=jnp.float32)


def local(
    tokens, w_qkv, w_out, w_up, w_down, ln1_gain, ln2_gain, kv_pool, page_table, lengths, moved
):
    rep_index = lax.axis_index("rep")
    row_index = lax.axis_index("row")
    seq = tokens.shape[2]
    share = tokens.shape[3]
    hidden_share = w_up.shape[1]
    head_width = D // H
    heads = share // head_width
    inputs = tokens.reshape(seq, share)
    spread_tokens = row_gather(inputs)
    shard = pack(jnp.swapaxes(w_qkv, 0, 1), w_up, w_down.T)
    weights = lax.all_gather(shard, ("z", "core"), axis=0, tiled=True)
    other = swapped(kv_pool, "rep", 0)
    out_block = lax.all_gather(w_out.T, "z", axis=0, tiled=False)
    out_block, spread_tokens, other = lax.optimization_barrier((out_block, spread_tokens, other))
    near = row_gather(out_block)
    rows = jnp.swapaxes(spread_tokens, 0, 1).reshape(seq, D)
    normed = normalize(rows.astype(jnp.float32), ln1_gain).astype(jnp.bfloat16)
    head_ids = (row_index * heads + jnp.arange(heads, dtype=jnp.int32) + 1).astype(jnp.float32)
    slopes = 2.0 ** (-8.0 * head_ids / H)

    def pages_of(store, table):
        return store[table].reshape(-1, store.shape[2])

    flag = moved[0] == 1
    home = jnp.where(flag, 1 - rep_index, rep_index)
    table = page_table[home, 0]
    length = lengths[home, 0]
    cache_keys = jnp.where(flag, pages_of(other[0, 0], table), pages_of(kv_pool[0, 0], table))
    cache_values = jnp.where(flag, pages_of(other[0, 1], table), pages_of(kv_pool[0, 1], table))
    attn_copies = attend(
        normed, weights, cache_keys, cache_values, length, slopes, lax.axis_size("row")
    )
    attns = row_exchange(attn_copies)
    near, _ = lax.optimization_barrier((near, attn_copies))
    far = swapped(near, "core", 0)
    place = jnp.stack([lax.axis_index("core"), row_index]).astype(jnp.int32)
    partial_down, state_local = feed(
        place, attns, spread_tokens, ln2_gain, near, far, weights, hidden_share
    )
    down = row_scatter_sum(partial_down)
    finished = (state_local.astype(jnp.float32) + down).astype(jnp.bfloat16)
    return finished.reshape(tokens.shape)


def solution(mesh):
    reps, rows, cols = mesh.devices.shape
    mesh = Mesh(mesh.devices.reshape(reps, rows, cols // 2, 2), ("rep", "row", "z", "core"))
    col = ("z", "core")
    return jax.shard_map(
        local,
        mesh=mesh,
        in_specs=(
            P("rep", col, None, "row"),
            P(col, None, "row"),
            P("row", col),
            P(col, "row"),
            P("row", col),
            P(),
            P(),
            P("rep", None, col, None, "row"),
            P(None, col, None),
            P(None, col),
            P(col),
        ),
        out_specs=P("rep", col, None, "row"),
        check_vma=False,
    )
```

```python
import math

import jax
import jax.numpy as jnp
from jax import lax
from jax.experimental import pallas as pl
from jax.experimental.pallas import tpu as pltpu
from jax.sharding import Mesh
from jax.sharding import PartitionSpec as P

D = 2048
H = 16
GROUPS = 4


def swapped(value, axis, apart):
    return lax.ppermute(value, axis, [(i, i ^ 1 << apart) for i in range(lax.axis_size(axis))])


def normalize(values, gain):
    mean = jnp.mean(values, axis=-1, keepdims=True)
    centred = values - mean
    spread = jnp.mean(centred * centred, axis=-1, keepdims=True)
    return centred * lax.rsqrt(spread + 1e-05) * gain


def attend_kernel(scalars, slopes, normed, weights, keys, values, copies, total, attn):
    step = pl.program_id(0)
    product = jnp.dot(normed[...], weights[...], preferred_element_type=jnp.float32)

    @pl.when(step == 0)
    def _():
        total[...] = product

    @pl.when(step > 0)
    def _():
        total[...] += product

    @pl.when(step == pl.num_programs(0) - 1)
    def _():
        length = scalars[0]
        seq = normed.shape[0]
        cached = keys.shape[0]
        share = keys.shape[1]
        head_width = D // H
        fold = jnp.float32(math.log2(math.e))
        scale = fold * jnp.float32(head_width) ** -0.5
        cache_pos = lax.broadcasted_iota(jnp.int32, (1, cached), 1)
        cache_ok = cache_pos < length
        cache_off = (cache_pos - length).astype(jnp.float32)
        new_pos = lax.broadcasted_iota(jnp.int32, (seq, seq), 1)
        new_ok = new_pos <= lax.broadcasted_iota(jnp.int32, (seq, seq), 0)
        new_off = lax.broadcasted_iota(jnp.int32, (1, seq), 1).astype(jnp.float32)
        for head in range(share // head_width):
            lanes = slice(head * head_width, (head + 1) * head_width)

            def part(index):
                start = index * share + head * head_width
                return total[:, start : start + head_width].astype(jnp.bfloat16)

            query, new_key, new_value = part(0), part(1), part(2)
            slope = fold * slopes[head]
            cache_bias = jnp.where(cache_ok, slope * cache_off, -1e30)
            cache_score = times_transposed(query, keys[:, lanes]) * scale + cache_bias
            new_score = times_transposed(query, new_key) * scale + slope * new_off
            new_score = jnp.where(new_ok, new_score, -1e30)
            top = jnp.maximum(
                jnp.max(cache_score, axis=1, keepdims=True),
                jnp.max(new_score, axis=1, keepdims=True),
            )
            cache_weight = jnp.exp2(cache_score - top)
            new_weight = jnp.exp2(new_score - top)
            whole = jnp.sum(cache_weight, axis=1, keepdims=True) + jnp.sum(
                new_weight, axis=1, keepdims=True
            )
            summed = jnp.dot(
                cache_weight.astype(jnp.bfloat16), values[:, lanes], preferred_element_type=jnp.float32
            ) + jnp.dot(new_weight.astype(jnp.bfloat16), new_value, preferred_element_type=jnp.float32)
            attn[:, lanes] = (summed / whole).astype(jnp.bfloat16)
        for row in range(copies.shape[0]):
            copies[row] = attn[...]


def attend(normed, weights, keys, values, length, slopes, rows):
    seq, width = normed.shape
    share = keys.shape[1]
    steps = 2
    deep = width // steps
    return pl.pallas_call(
        attend_kernel,
        out_shape=jax.ShapeDtypeStruct((rows, seq, share), jnp.bfloat16),
        grid_spec=pltpu.PrefetchScalarGridSpec(
            num_scalar_prefetch=2,
            grid=(steps,),
            in_specs=[
                pl.BlockSpec((seq, deep), lambda k, *_: (0, k)),
                pl.BlockSpec((deep, 3 * share), lambda k, *_: (k, 0)),
                pl.BlockSpec(keys.shape, lambda k, *_: (0, 0)),
                pl.BlockSpec(values.shape, lambda k, *_: (0, 0)),
            ],
            out_specs=pl.BlockSpec((rows, seq, share), lambda k, *_: (0, 0, 0)),
            scratch_shapes=[
                pltpu.VMEM((seq, 3 * share), jnp.float32),
                pltpu.VMEM((seq, share), jnp.bfloat16),
            ],
        ),
        compiler_params=pltpu.CompilerParams(vmem_limit_bytes=48 << 20),
    )(length.reshape(1), slopes, normed, weights, keys, values)


def feed_kernel(place, attns, tokens, gain, near, far, gathered, down, state_local,
                out_weights, feed_weights, wide, state, hidden, sems):
    rows, seq, share = attns.shape
    width = rows * share
    hidden_share = feed_weights.shape[2]
    chips = near.shape[1]
    first = 3 * share
    copies = []

    def copy(source, target):
        copies.append(pltpu.make_async_copy(source, target, sems.at[len(copies)]))
        copies[-1].start()

    span = chips // GROUPS
    for group in range(GROUPS):
        picked = pl.ds(group * span, span)
        for row in range(rows):
            lanes = pl.ds(row * share, share)
            copy(near.at[row, picked], out_weights.at[picked, place[0], :, lanes])
            copy(far.at[row, picked], out_weights.at[picked, 1 - place[0], :, lanes])
    for part in range(2):
        copy(gathered.at[:, pl.ds(first + part * hidden_share, hidden_share)], feed_weights.at[part])
    for row in range(rows):
        wide[:, row * share : (row + 1) * share] = attns[row]
    each = chips // rows
    for row in range(rows):
        if row % (rows // GROUPS) == 0:
            group = row // (rows // GROUPS)
            for item in copies[2 * rows * group : 2 * rows * (group + 1)]:
                item.wait()
        block = out_weights[row * each : (row + 1) * each].reshape(share, width)
        mixed = times_transposed(wide[...], block)
        state[row] = (tokens[row].astype(jnp.float32) + mixed).astype(jnp.bfloat16)
    state_local[...] = state[place[1]]
    pieces = [state[row].astype(jnp.float32) for row in range(rows)]
    mean = sum(jnp.sum(piece, axis=1, keepdims=True) for piece in pieces) / width
    centred = [piece - mean for piece in pieces]
    spread = sum(jnp.sum(piece * piece, axis=1, keepdims=True) for piece in centred) / width
    factor = lax.rsqrt(spread + 1e-05)
    for row in range(rows):
        lanes = slice(row * share, (row + 1) * share)
        wide[:, lanes] = (centred[row] * factor * gain[:, lanes]).astype(jnp.bfloat16)
    copies[-2].wait()
    for part in range(4):
        lanes = slice(part * hidden_share // 4, (part + 1) * hidden_share // 4)
        up = jnp.dot(wide[...], feed_weights[0, :, lanes], preferred_element_type=jnp.float32)
        hidden[:, lanes] = jax.nn.gelu(up, approximate=True).astype(jnp.bfloat16)
    copies[-1].wait()
    for row in range(rows):
        lanes = slice(row * share, (row + 1) * share)
        down[row] = times_transposed(hidden[...], feed_weights[1, lanes, :]).astype(jnp.bfloat16)


def feed(place, attns, tokens, gain, near, far, gathered, hidden_share):
    rows, seq, share = attns.shape
    width = rows * share
    chips = near.shape[1]
    return pl.pallas_call(
        feed_kernel,
        out_shape=(
            jax.ShapeDtypeStruct(attns.shape, jnp.bfloat16),
            jax.ShapeDtypeStruct((seq, share), jnp.bfloat16),
        ),
        grid_spec=pltpu.PrefetchScalarGridSpec(
            num_scalar_prefetch=1,
            grid=(1,),
            in_specs=[
                pl.BlockSpec(attns.shape, lambda *_: (0, 0, 0)),
                pl.BlockSpec(tokens.shape, lambda *_: (0, 0, 0)),
                pl.BlockSpec((1, width), lambda *_: (0, 0)),
                pl.BlockSpec(memory_space=pl.ANY),
                pl.BlockSpec(memory_space=pl.ANY),
                pl.BlockSpec(memory_space=pl.ANY),
            ],
            out_specs=(
                pl.BlockSpec(attns.shape, lambda *_: (0, 0, 0)),
                pl.BlockSpec((seq, share), lambda *_: (0, 0)),
            ),
            scratch_shapes=[
                pltpu.VMEM((chips, 2, width // chips // 2, width), jnp.bfloat16),
                pltpu.VMEM((2, width, hidden_share), jnp.bfloat16),
                pltpu.VMEM((seq, width), jnp.bfloat16),
                pltpu.VMEM(attns.shape, jnp.bfloat16),
                pltpu.VMEM((seq, hidden_share), jnp.bfloat16),
                pltpu.SemaphoreType.DMA((2 * rows * GROUPS + 2,)),
            ],
        ),
        compiler_params=pltpu.CompilerParams(vmem_limit_bytes=48 << 20),
    )(place, attns, tokens, gain.reshape(1, width), near, far, gathered)


def pack_kernel(qkv, up, down, tokens, shard, copies, sems):
    moves = [
        pltpu.make_async_copy(tokens, copies.at[row], sems.at[row]) for row in range(copies.shape[0])
    ]
    for move in moves:
        move.start()
    start = 0
    for source in [qkv.at[part] for part in range(qkv.shape[0])] + [up, down]:
        shard[:, start : start + source.shape[1]] = source[...]
        start += source.shape[1]
    for move in moves:
        move.wait()


def pack(qkv, up, down, tokens, size):
    parts, rows, share = qkv.shape
    width = parts * share + up.shape[1] + down.shape[1]
    on_chip = pl.BlockSpec(memory_space=pltpu.VMEM)
    return pl.pallas_call(
        pack_kernel,
        out_shape=(
            jax.ShapeDtypeStruct((rows, width), jnp.bfloat16),
            jax.ShapeDtypeStruct((size,) + tokens.shape, jnp.bfloat16),
        ),
        in_specs=[on_chip] * 4,
        out_specs=(on_chip, pl.BlockSpec(memory_space=pl.ANY)),
        scratch_shapes=[pltpu.SemaphoreType.DMA((size,))],
    )(qkv, up, down, tokens)


def row_exchange(parts):
    return lax.all_to_all(parts, "row", 0, 0, tiled=True)


def row_gather(value):
    return row_exchange(jnp.broadcast_to(value[None], (lax.axis_size("row"),) + value.shape))


def row_scatter_sum(parts):
    parts = row_exchange(parts)
    return jnp.sum(parts.astype(jnp.float32), axis=0)


def times_transposed(left, right):
    return lax.dot_general(left, right, (((1,), (1,)), ((), ())), preferred_element_type=jnp.float32)


def local(
    tokens, w_qkv, w_out, w_up, w_down, ln1_gain, ln2_gain, kv_pool, page_table, lengths, moved
):
    rep_index = lax.axis_index("rep")
    row_index = lax.axis_index("row")
    seq = tokens.shape[2]
    share = tokens.shape[3]
    hidden_share = w_up.shape[1]
    head_width = D // H
    heads = share // head_width
    inputs = tokens.reshape(seq, share)
    shard, token_copies = pack(
        jnp.swapaxes(w_qkv, 0, 1), w_up, w_down.T, inputs, lax.axis_size("row")
    )
    spread_tokens = row_exchange(token_copies)
    weights = lax.all_gather(shard, ("z", "core"), axis=0, tiled=True)
    other = swapped(kv_pool, "rep", 0)
    out_block = lax.all_gather(w_out.T, "z", axis=0, tiled=False)
    out_block, spread_tokens, other = lax.optimization_barrier((out_block, spread_tokens, other))
    near = row_gather(out_block)
    rows = jnp.swapaxes(spread_tokens, 0, 1).reshape(seq, D)
    normed = normalize(rows.astype(jnp.float32), ln1_gain).astype(jnp.bfloat16)
    head_ids = (row_index * heads + jnp.arange(heads, dtype=jnp.int32) + 1).astype(jnp.float32)
    slopes = 2.0 ** (-8.0 * head_ids / H)

    def pages_of(store, table):
        return store[table].reshape(-1, store.shape[2])

    flag = moved[0] == 1
    home = jnp.where(flag, 1 - rep_index, rep_index)
    table = page_table[home, 0]
    length = lengths[home, 0]
    cache_keys = jnp.where(flag, pages_of(other[0, 0], table), pages_of(kv_pool[0, 0], table))
    cache_values = jnp.where(flag, pages_of(other[0, 1], table), pages_of(kv_pool[0, 1], table))
    attn_copies = attend(
        normed, weights, cache_keys, cache_values, length, slopes, lax.axis_size("row")
    )
    attns = row_exchange(attn_copies)
    near, _ = lax.optimization_barrier((near, attn_copies))
    far = swapped(near, "core", 0)
    place = jnp.stack([lax.axis_index("core"), row_index]).astype(jnp.int32)
    partial_down, state_local = feed(
        place, attns, spread_tokens, ln2_gain, near, far, weights, hidden_share
    )
    down = row_scatter_sum(partial_down)
    finished = (state_local.astype(jnp.float32) + down).astype(jnp.bfloat16)
    return finished.reshape(tokens.shape)


def solution(mesh):
    reps, rows, cols = mesh.devices.shape
    mesh = Mesh(mesh.devices.reshape(reps, rows, cols // 2, 2), ("rep", "row", "z", "core"))
    col = ("z", "core")
    return jax.shard_map(
        local,
        mesh=mesh,
        in_specs=(
            P("rep", col, None, "row"),
            P(col, None, "row"),
            P("row", col),
            P(col, "row"),
            P("row", col),
            P(),
            P(),
            P("rep", None, col, None, "row"),
            P(None, col, None),
            P(None, col),
            P(col),
        ),
        out_specs=P("rep", col, None, "row"),
        check_vma=False,
    )
```

```python
import math

import jax
import jax.numpy as jnp
from jax import lax
from jax.experimental import pallas as pl
from jax.experimental.pallas import tpu as pltpu
from jax.sharding import Mesh
from jax.sharding import PartitionSpec as P

D = 2048
H = 16
GROUPS = 4


def swapped(value, axis, apart):
    return lax.ppermute(value, axis, [(i, i ^ 1 << apart) for i in range(lax.axis_size(axis))])


def normalize(values, gain):
    mean = jnp.mean(values, axis=-1, keepdims=True)
    centred = values - mean
    spread = jnp.mean(centred * centred, axis=-1, keepdims=True)
    return centred * lax.rsqrt(spread + 1e-05) * gain


def attend_kernel(scalars, slopes, normed, weights, keys, values, _, copies, total, attn):
    step = pl.program_id(0)
    product = jnp.dot(normed[...], weights[...], preferred_element_type=jnp.float32)

    @pl.when(step == 0)
    def _():
        total[...] = product

    @pl.when(step > 0)
    def _():
        total[...] += product

    @pl.when(step == pl.num_programs(0) - 1)
    def _():
        length = scalars[0]
        seq = normed.shape[0]
        cached = keys.shape[0]
        share = keys.shape[1]
        head_width = D // H
        fold = jnp.float32(math.log2(math.e))
        scale = fold * jnp.float32(head_width) ** -0.5
        cache_pos = lax.broadcasted_iota(jnp.int32, (1, cached), 1)
        cache_ok = cache_pos < length
        cache_off = (cache_pos - length).astype(jnp.float32)
        new_pos = lax.broadcasted_iota(jnp.int32, (seq, seq), 1)
        new_ok = new_pos <= lax.broadcasted_iota(jnp.int32, (seq, seq), 0)
        new_off = lax.broadcasted_iota(jnp.int32, (1, seq), 1).astype(jnp.float32)
        for head in range(share // head_width):
            lanes = slice(head * head_width, (head + 1) * head_width)

            def part(index):
                start = index * share + head * head_width
                return total[:, start : start + head_width].astype(jnp.bfloat16)

            query, new_key, new_value = part(0), part(1), part(2)
            slope = fold * slopes[head]
            cache_bias = jnp.where(cache_ok, slope * cache_off, -1e30)
            cache_score = times_transposed(query, keys[:, lanes]) * scale + cache_bias
            new_score = times_transposed(query, new_key) * scale + slope * new_off
            new_score = jnp.where(new_ok, new_score, -1e30)
            top = jnp.maximum(
                jnp.max(cache_score, axis=1, keepdims=True),
                jnp.max(new_score, axis=1, keepdims=True),
            )
            cache_weight = jnp.exp2(cache_score - top)
            new_weight = jnp.exp2(new_score - top)
            whole = jnp.sum(cache_weight, axis=1, keepdims=True) + jnp.sum(
                new_weight, axis=1, keepdims=True
            )
            summed = jnp.dot(
                cache_weight.astype(jnp.bfloat16), values[:, lanes], preferred_element_type=jnp.float32
            ) + jnp.dot(new_weight.astype(jnp.bfloat16), new_value, preferred_element_type=jnp.float32)
            attn[:, lanes] = (summed / whole).astype(jnp.bfloat16)
        for row in range(copies.shape[0]):
            copies[row] = attn[...]


def attend(normed, weights, keys, values, arrived, length, slopes, rows):
    seq, width = normed.shape
    share = keys.shape[1]
    steps = 2
    deep = width // steps
    return pl.pallas_call(
        attend_kernel,
        out_shape=jax.ShapeDtypeStruct((rows, seq, share), jnp.bfloat16),
        grid_spec=pltpu.PrefetchScalarGridSpec(
            num_scalar_prefetch=2,
            grid=(steps,),
            in_specs=[
                pl.BlockSpec((seq, deep), lambda k, *_: (0, k)),
                pl.BlockSpec((deep, 3 * share), lambda k, *_: (k, 0)),
                pl.BlockSpec(keys.shape, lambda k, *_: (0, 0)),
                pl.BlockSpec(values.shape, lambda k, *_: (0, 0)),
                pl.BlockSpec(memory_space=pl.ANY),
            ],
            out_specs=pl.BlockSpec((rows, seq, share), lambda k, *_: (0, 0, 0)),
            scratch_shapes=[
                pltpu.VMEM((seq, 3 * share), jnp.float32),
                pltpu.VMEM((seq, share), jnp.bfloat16),
            ],
        ),
        compiler_params=pltpu.CompilerParams(vmem_limit_bytes=48 << 20),
    )(length.reshape(1), slopes, normed, weights, keys, values, arrived)


def feed_kernel(place, attns, tokens, gain, near, far, gathered, down, state_local,
                out_weights, feed_weights, wide, state, hidden, sems):
    rows, seq, share = attns.shape
    width = rows * share
    hidden_share = feed_weights.shape[2]
    chips = near.shape[1]
    first = 3 * share
    copies = []

    def copy(source, target):
        copies.append(pltpu.make_async_copy(source, target, sems.at[len(copies)]))
        copies[-1].start()

    span = chips // GROUPS
    for group in range(GROUPS):
        picked = pl.ds(group * span, span)
        for row in range(rows):
            lanes = pl.ds(row * share, share)
            copy(near.at[row, picked], out_weights.at[picked, place[0], :, lanes])
            copy(far.at[row, picked], out_weights.at[picked, 1 - place[0], :, lanes])
    for part in range(2):
        copy(gathered.at[:, pl.ds(first + part * hidden_share, hidden_share)], feed_weights.at[part])
    for row in range(rows):
        wide[:, row * share : (row + 1) * share] = attns[row]
    each = chips // rows
    for row in range(rows):
        if row % (rows // GROUPS) == 0:
            group = row // (rows // GROUPS)
            for item in copies[2 * rows * group : 2 * rows * (group + 1)]:
                item.wait()
        block = out_weights[row * each : (row + 1) * each].reshape(share, width)
        mixed = times_transposed(wide[...], block)
        state[row] = (tokens[row].astype(jnp.float32) + mixed).astype(jnp.bfloat16)
    state_local[...] = state[place[1]]
    pieces = [state[row].astype(jnp.float32) for row in range(rows)]
    mean = sum(jnp.sum(piece, axis=1, keepdims=True) for piece in pieces) / width
    centred = [piece - mean for piece in pieces]
    spread = sum(jnp.sum(piece * piece, axis=1, keepdims=True) for piece in centred) / width
    factor = lax.rsqrt(spread + 1e-05)
    for row in range(rows):
        lanes = slice(row * share, (row + 1) * share)
        wide[:, lanes] = (centred[row] * factor * gain[:, lanes]).astype(jnp.bfloat16)
    copies[-2].wait()
    for part in range(4):
        lanes = slice(part * hidden_share // 4, (part + 1) * hidden_share // 4)
        up = jnp.dot(wide[...], feed_weights[0, :, lanes], preferred_element_type=jnp.float32)
        hidden[:, lanes] = jax.nn.gelu(up, approximate=True).astype(jnp.bfloat16)
    copies[-1].wait()
    for row in range(rows):
        lanes = slice(row * share, (row + 1) * share)
        down[row] = times_transposed(hidden[...], feed_weights[1, lanes, :]).astype(jnp.bfloat16)


def feed(place, attns, tokens, gain, near, far, gathered, hidden_share):
    rows, seq, share = attns.shape
    width = rows * share
    chips = near.shape[1]
    return pl.pallas_call(
        feed_kernel,
        out_shape=(
            jax.ShapeDtypeStruct(attns.shape, jnp.bfloat16),
            jax.ShapeDtypeStruct((seq, share), jnp.bfloat16),
        ),
        grid_spec=pltpu.PrefetchScalarGridSpec(
            num_scalar_prefetch=1,
            grid=(1,),
            in_specs=[
                pl.BlockSpec(attns.shape, lambda *_: (0, 0, 0)),
                pl.BlockSpec(tokens.shape, lambda *_: (0, 0, 0)),
                pl.BlockSpec((1, width), lambda *_: (0, 0)),
                pl.BlockSpec(memory_space=pl.ANY),
                pl.BlockSpec(memory_space=pl.ANY),
                pl.BlockSpec(memory_space=pl.ANY),
            ],
            out_specs=(
                pl.BlockSpec(attns.shape, lambda *_: (0, 0, 0)),
                pl.BlockSpec((seq, share), lambda *_: (0, 0)),
            ),
            scratch_shapes=[
                pltpu.VMEM((chips, 2, width // chips // 2, width), jnp.bfloat16),
                pltpu.VMEM((2, width, hidden_share), jnp.bfloat16),
                pltpu.VMEM((seq, width), jnp.bfloat16),
                pltpu.VMEM(attns.shape, jnp.bfloat16),
                pltpu.VMEM((seq, hidden_share), jnp.bfloat16),
                pltpu.SemaphoreType.DMA((2 * rows * GROUPS + 2,)),
            ],
        ),
        compiler_params=pltpu.CompilerParams(vmem_limit_bytes=48 << 20),
    )(place, attns, tokens, gain.reshape(1, width), near, far, gathered)


def pack_kernel(qkv, up, down, tokens, shard, copies, sems):
    moves = [
        pltpu.make_async_copy(tokens, copies.at[row], sems.at[row]) for row in range(copies.shape[0])
    ]
    for move in moves:
        move.start()
    start = 0
    for source in [qkv.at[part] for part in range(qkv.shape[0])] + [up, down]:
        shard[:, start : start + source.shape[1]] = source[...]
        start += source.shape[1]
    for move in moves:
        move.wait()


def pack(qkv, up, down, tokens, size):
    parts, rows, share = qkv.shape
    width = parts * share + up.shape[1] + down.shape[1]
    on_chip = pl.BlockSpec(memory_space=pltpu.VMEM)
    return pl.pallas_call(
        pack_kernel,
        out_shape=(
            jax.ShapeDtypeStruct((rows, width), jnp.bfloat16),
            jax.ShapeDtypeStruct((size,) + tokens.shape, jnp.bfloat16),
        ),
        in_specs=[on_chip] * 4,
        out_specs=(on_chip, pl.BlockSpec(memory_space=pl.ANY)),
        scratch_shapes=[pltpu.SemaphoreType.DMA((size,))],
    )(qkv, up, down, tokens)


def row_exchange(parts):
    return lax.all_to_all(parts, "row", 0, 0, tiled=True)


def row_gather(value):
    return row_exchange(jnp.broadcast_to(value[None], (lax.axis_size("row"),) + value.shape))


def row_scatter_sum(parts):
    parts = row_exchange(parts)
    return jnp.sum(parts.astype(jnp.float32), axis=0)


def times_transposed(left, right):
    return lax.dot_general(left, right, (((1,), (1,)), ((), ())), preferred_element_type=jnp.float32)


def local(
    tokens, w_qkv, w_out, w_up, w_down, ln1_gain, ln2_gain, kv_pool, page_table, lengths, moved
):
    rep_index = lax.axis_index("rep")
    row_index = lax.axis_index("row")
    seq = tokens.shape[2]
    share = tokens.shape[3]
    hidden_share = w_up.shape[1]
    head_width = D // H
    heads = share // head_width
    inputs = tokens.reshape(seq, share)
    shard, token_copies = pack(
        jnp.swapaxes(w_qkv, 0, 1), w_up, w_down.T, inputs, lax.axis_size("row")
    )
    spread_tokens = row_exchange(token_copies)
    weights = lax.all_gather(shard, ("z", "core"), axis=0, tiled=True)
    other = swapped(kv_pool, "rep", 0)
    out_block = lax.all_gather(w_out.T, "z", axis=0, tiled=False)
    arrived = other[0, 0, 0, :16, :128]
    out_block, spread_tokens, arrived = lax.optimization_barrier((out_block, spread_tokens, arrived))
    near = row_gather(out_block)
    rows = jnp.swapaxes(spread_tokens, 0, 1).reshape(seq, D)
    normed = normalize(rows.astype(jnp.float32), ln1_gain).astype(jnp.bfloat16)
    head_ids = (row_index * heads + jnp.arange(heads, dtype=jnp.int32) + 1).astype(jnp.float32)
    slopes = 2.0 ** (-8.0 * head_ids / H)

    def pages_of(store, table):
        return store[table].reshape(-1, store.shape[2])

    flag = moved[0] == 1
    home = jnp.where(flag, 1 - rep_index, rep_index)
    table = page_table[home, 0]
    length = lengths[home, 0]
    cache_keys = jnp.where(flag, pages_of(other[0, 0], table), pages_of(kv_pool[0, 0], table))
    cache_values = jnp.where(flag, pages_of(other[0, 1], table), pages_of(kv_pool[0, 1], table))
    attn_copies = attend(
        normed, weights, cache_keys, cache_values, arrived, length, slopes, lax.axis_size("row")
    )
    attns = row_exchange(attn_copies)
    near, _ = lax.optimization_barrier((near, attn_copies))
    far = swapped(near, "core", 0)
    place = jnp.stack([lax.axis_index("core"), row_index]).astype(jnp.int32)
    partial_down, state_local = feed(
        place, attns, spread_tokens, ln2_gain, near, far, weights, hidden_share
    )
    down = row_scatter_sum(partial_down)
    finished = (state_local.astype(jnp.float32) + down).astype(jnp.bfloat16)
    return finished.reshape(tokens.shape)


def solution(mesh):
    reps, rows, cols = mesh.devices.shape
    mesh = Mesh(mesh.devices.reshape(reps, rows, cols // 2, 2), ("rep", "row", "z", "core"))
    col = ("z", "core")
    return jax.shard_map(
        local,
        mesh=mesh,
        in_specs=(
            P("rep", col, None, "row"),
            P(col, None, "row"),
            P("row", col),
            P(col, "row"),
            P("row", col),
            P(),
            P(),
            P("rep", None, col, None, "row"),
            P(None, col, None),
            P(None, col),
            P(col),
        ),
        out_specs=P("rep", col, None, "row"),
        check_vma=False,
    )
```
